32 devices in a mesh: grp: 2 (over y), frm: 4 (over z), row: 4 (over x, core).
Axes of the slice: x: 2, y: 2, z: 4, core: 2. Of those that a mesh axis runs over, the one named last changes fastest.
Arguments:
- queries: bfloat16 [16, 8, 128, 2240], P(('grp', 'frm'), 'row'), parts along dimension 0, may hold values from -6 to 6
- keys: bfloat16 [16, 8, 128, 2240], P(('grp', 'frm'), 'row'), parts along dimension 0, may hold values from -6 to 6
- values: bfloat16 [16, 8, 128, 2240], P(('grp', 'frm'), 'row'), parts along dimension 0, may hold values from -6 to 6
- flags: int32 [16], P(('grp', 'frm')), parts along dimension 0, may hold values 0 or 1
- blocks: int32 [16], P(('grp', 'frm')), parts along dimension 0, may hold values from 0 to 2, as said below
- out_weight: bfloat16 [2240, 2240], P('frm'), may hold values from -0.125 to 0.125
- norm_gain: float32 [2240], replicated, may hold values from 0.1 to 1.9
Outputs:
- projected: bfloat16 [16, 8, 128, 2240], P(('grp', 'frm'), 'row'), parts along dimension 0
The draws below stay inside these ranges and needn't reach their ends.
There are 2 independent parts, one for each index of `grp`. The reference program is written for one: setup_inputs(seed, part) draws one part's arguments, and reference() takes and returns one part's arrays. A program takes and returns all parts, laid end to end along the dimension named above; an argument that names none is the same for every part. Nothing has to cross between parts.
Inputs may be any that keep to these rules, and one draw needn't show every extreme that they name: `flags`: 1 marks a clean frame, 0 a noisy one. `blocks`: within the 8 frames of one group, block numbers never fall and each block is 1 to 4 consecutive frames, some block exactly 4; every number from 0 to 2 occurs.
All inputs are finite; a program needn't handle non-finite values. No bound on the sum of `flags` on one device may be relied on, other than what follows from the above.
Results may differ from the reference program's by a relative error of at most 0.0049.
Values may be sent and summed in bfloat16 or wider, within the bound.
No kernel may reach another device: no remote copies, remote signals or barrier semaphores. Data moves between devices by JAX's collectives and lax.ppermute only.
A program may use at most 192 MiB of HBM per device.

```python
import jax
import jax.numpy as jnp
from jax import lax

HEADS = 20
HD = 112
D = 2240
WL = 128
FRAMES = 8
HL = 8
BLOCKS = 3


def draw_blocks(key, part):
    base_key = jax.random.fold_in(key, 7301)
    first_key, loop_key = jax.random.split(base_key)
    chosen = jax.random.randint(first_key, (), 0, BLOCKS)
    positions = jnp.arange(BLOCKS, dtype=jnp.int32)
    lengths = jnp.ones((BLOCKS,), jnp.int32) + 3 * (positions == chosen).astype(jnp.int32)
    remain = FRAMES - BLOCKS - 3

    def place_one(step, current):
        step_key = jax.random.fold_in(loop_key, step)
        priority = jax.random.permutation(step_key, BLOCKS).astype(jnp.int32)
        scores = jnp.where(current < 4, priority, -1)
        target = jnp.argmax(scores)
        return current + (positions == target).astype(jnp.int32)
    lengths = lax.fori_loop(0, remain, place_one, lengths)
    ends = jnp.cumsum(lengths).astype(jnp.int32)
    frame_pos = jnp.arange(FRAMES, dtype=jnp.int32)
    return jnp.sum((ends[None, :] <= frame_pos[:, None]).astype(jnp.int32), axis=1).astype(jnp.int32)


def set_ends(values, key, smallest, largest):
    dims = values.shape
    index_at = [jax.random.randint(jax.random.fold_in(key, axis), (), 0, dims[axis]) for axis in range(len(dims))]
    values = values.at[tuple(index_at)].set(smallest)
    longest = dims.index(max(dims))
    index_at[longest] = (index_at[longest] + 1) % dims[longest]
    return values.at[tuple(index_at)].set(largest)


def block_scale(key, extent, cuts, smallest, largest):
    level, own = 1.0, jax.random.fold_in(key, 6)
    for axis_at, parts in cuts:
        steps = jnp.exp(jax.random.uniform(jax.random.fold_in(own, axis_at), (parts,), jnp.float32, smallest / len(cuts), largest / len(cuts)))
        level = level * jnp.repeat(steps, extent[axis_at] // parts).reshape([-1 if axis == axis_at else 1 for axis in range(len(extent))])
    return level


def bell_draw(rng, extent, deviation, most, shards=(), kind=jnp.bfloat16):
    factor_of = block_scale(rng, extent, shards, -0.22, 0.18) if shards else 1.0
    drawn = jax.random.normal(rng, extent, jnp.float32) * deviation * factor_of
    return jnp.minimum(jnp.maximum(drawn, -most), most).astype(kind)


def setup_inputs(seed: int = 0, part: int = 0) -> dict:
    seeds = jax.random.split(jax.random.key(seed), 8)
    part_splits = jax.random.split(jax.random.fold_in(seeds[7], part), 8)
    queries = bell_draw(part_splits[0], (FRAMES, HL, WL, D), 1.0, 6.0, ((0, 4), (1, 4)))
    keys = bell_draw(part_splits[1], (FRAMES, HL, WL, D), 1.0, 6.0, ((0, 4), (1, 4)))
    values = bell_draw(part_splits[2], (FRAMES, HL, WL, D), 1.0, 6.0, ((0, 4), (1, 4)))
    flags = set_ends((jax.random.randint(part_splits[3], (FRAMES,), 0, 2) < 1).astype(jnp.int32), jax.random.fold_in(part_splits[3], 1), 0, 1)
    blocks = draw_blocks(jax.random.fold_in(jax.random.fold_in(seeds[7], part), 71), part)
    out_weight = bell_draw(seeds[5], (D, D), D ** -0.5, 0.125, ((0, 4),))
    norm_gain = jnp.clip(1.0 + 0.18 * jax.random.normal(seeds[6], (D,), jnp.float32), 0.1, 1.9)
    return dict(queries=queries, keys=keys, values=values, flags=flags, blocks=blocks, out_weight=out_weight, norm_gain=norm_gain)


norm_eps = 1e-06

def reference(queries, keys, values, flags, blocks, out_weight, norm_gain):
    frames, lat_rows, lat_cols, model_width = queries.shape
    tokens = lat_rows * lat_cols
    weight_full = out_weight.astype(jnp.float32)
    gain_table = norm_gain.astype(jnp.float32).reshape(HEADS, HD)

    def frame_step(carried, inputs):
        closed, opened, latest = carried
        query_frame, key_frame, value_frame, flag_frame, block_frame = inputs
        key_pos = jax.nn.relu(key_frame).reshape(tokens, HEADS, HD).astype(jnp.float32)
        value_heads = value_frame.reshape(tokens, HEADS, HD).astype(jnp.float32)
        frame_state = jnp.einsum('tha,thb->hab', key_pos, value_heads, precision=lax.Precision.HIGHEST)
        flag_value = flag_frame.astype(jnp.float32)
        block_value = block_frame.astype(jnp.float32)
        advance = (latest < block_value).astype(jnp.float32)
        select = jnp.maximum(advance, flag_value)
        read_state = closed + select * opened + frame_state
        query_pos = jax.nn.relu(query_frame).reshape(tokens, HEADS, HD).astype(jnp.float32)
        attended = jnp.einsum('tha,hab->thb', query_pos, read_state, precision=lax.Precision.HIGHEST)
        inv_rms = lax.rsqrt(lax.optimization_barrier(jnp.mean(attended * attended, axis=-1, keepdims=True)) + norm_eps)
        normed = (attended * inv_rms * gain_table).astype(jnp.bfloat16).reshape(tokens, model_width)
        projected = jnp.dot(normed.astype(jnp.float32), weight_full, precision=lax.Precision.HIGHEST)
        projected = projected.astype(jnp.bfloat16).reshape(lat_rows, lat_cols, model_width)
        new_carry = (closed + advance * opened, flag_value * frame_state + (1.0 - advance) * opened, jnp.maximum(latest, block_value))
        return (new_carry, projected)
    initial = (jnp.zeros((HEADS, HD, HD), jnp.float32), jnp.zeros((HEADS, HD, HD), jnp.float32), jnp.array(-1.0, jnp.float32))
    _, outputs = lax.scan(frame_step, initial, (queries, keys, values, flags, blocks))
    return outputs
```

```python
import functools

import jax
import jax.numpy as jnp
from jax import lax
from jax.experimental import pallas as pl
from jax.experimental.pallas import tpu as pltpu
from jax.sharding import PartitionSpec as P


HEADS = 20
HD = 112

norm_eps = 1e-06

STATES_VMEM = 64843328
SMALL_VMEM = 8 << 20
PROJECT_VMEM = 36 << 20
LANES = 128
LOADS = 4
BAND = 768


def ring(size, shift):
    return [(i, (i + shift) % size) for i in range(size)]


def side_by_side(ref, frame, rows):
    return jnp.concatenate([ref[frame, r, rows, :] for r in range(ref.shape[1])], axis=1)


def state_kernel(chips, heads_per, k_ref, v_ref, own_ref, sent_ref, *scratch):
    keys, values, exact, rounded, load_sem, sem = scratch
    row = lax.axis_index("row")
    chip, core = row // 2, lax.rem(row, 2)
    frames, _, width, _ = keys.shape
    per = width // LOADS
    loads = []
    for frame in range(frames):
        for part in range(LOADS):
            at = pl.ds(part * per, per)
            loads.append(
                [
                    pltpu.make_async_copy(
                        ref.at[frame, :, at], held.at[frame, :, at], load_sem.at[n, frame, part]
                    )
                    for n, (ref, held) in enumerate(((k_ref, keys), (v_ref, values)))
                ]
            )
    for pair in loads:
        for load in pair:
            load.start()
    for frame in range(frames):
        for head in range(HEADS):
            if head * HD % per == 0:
                for load in loads[frame * LOADS + head * HD // per]:
                    load.wait()
            at = slice(head * HD, (head + 1) * HD)
            state = lax.dot_general(
                side_by_side(values, frame, at),
                jnp.maximum(side_by_side(keys, frame, at), 0),
                (((1,), (1,)), ((), ())),
                preferred_element_type=jnp.float32,
            )
            exact[frame, head] = state
            rounded[frame, head] = state.astype(jnp.bfloat16)
        for head in range(HEADS, exact.shape[1]):
            exact[frame, head] = jnp.zeros((HD, HD), jnp.float32)
            rounded[frame, head] = jnp.zeros((HD, HD), jnp.bfloat16)
    copies = []
    for frame in range(frames):
        for step in range(chips):
            other = lax.rem(chip + step, chips) * 2
            mine = pl.ds((other + core) * heads_per, heads_per)
            theirs = pl.ds((other + 1 - core) * heads_per, heads_per)
            copies.append(
                pltpu.make_async_copy(
                    rounded.at[frame, theirs], sent_ref.at[step, frame], sem.at[1, frame, step]
                )
            )
            copies.append(
                pltpu.make_async_copy(
                    exact.at[frame, mine], own_ref.at[step, frame], sem.at[0, frame, step]
                )
            )
    for copy in copies:
        copy.start()
    for copy in copies:
        copy.wait()


def partial_states(keys, values, rows, heads_per):
    frames, _, _, _ = keys.shape
    chips = rows // 2
    far = pl.BlockSpec(memory_space=pltpu.MemorySpace.HBM)
    anywhere = pl.BlockSpec(memory_space=pl.ANY)
    piece = (chips, frames, heads_per, HD, HD)
    held = (frames, rows * heads_per, HD, HD)
    return pl.pallas_call(
        functools.partial(state_kernel, chips, heads_per),
        in_specs=[far, far],
        out_specs=[anywhere] * 2,
        scratch_shapes=[
            pltpu.VMEM(keys.shape, jnp.bfloat16),
            pltpu.VMEM(keys.shape, jnp.bfloat16),
            pltpu.VMEM(held, jnp.float32),
            pltpu.VMEM(held, jnp.bfloat16),
            pltpu.SemaphoreType.DMA((2, frames, LOADS)),
            pltpu.SemaphoreType.DMA((2, frames, chips)),
        ],
        out_shape=[
            jax.ShapeDtypeStruct(piece, jnp.float32),
            jax.ShapeDtypeStruct(piece, jnp.bfloat16),
        ],
        cost_estimate=pl.CostEstimate(
            flops=2 * keys.size * HD * 8, bytes_accessed=4 * keys.size, transcendentals=0
        ),
        compiler_params=pltpu.CompilerParams(vmem_limit_bytes=STATES_VMEM),
        name="states",
    )(keys, values)


def small(body, scalars, arrays, outs):
    scalar = pl.BlockSpec(memory_space=pltpu.SMEM)
    whole = pl.BlockSpec(memory_space=pltpu.VMEM)
    moved_bytes = sum(a.size * a.dtype.itemsize for a in arrays)
    return pl.pallas_call(
        body,
        in_specs=[scalar] * len(scalars) + [whole] * len(arrays),
        out_specs=[whole] * len(outs),
        out_shape=outs,
        cost_estimate=pl.CostEstimate(
            flops=moved_bytes, bytes_accessed=2 * moved_bytes, transcendentals=0
        ),
        compiler_params=pltpu.CompilerParams(vmem_limit_bytes=SMALL_VMEM),
    )(*scalars, *arrays)


def pair_kernel(own_ref, got_ref, mine_ref, *sent_refs):
    mine_ref[...] = own_ref[0] + got_ref[0].astype(jnp.float32)
    for step, sent_ref in enumerate(sent_refs, 1):
        total = own_ref[step] + got_ref[step].astype(jnp.float32)
        sent_ref[...] = total.astype(jnp.bfloat16)


def add_pair(own, got):
    shape = own.shape[1:]
    outs = [jax.ShapeDtypeStruct(shape, jnp.float32)]
    outs += [jax.ShapeDtypeStruct(shape, jnp.bfloat16)] * (own.shape[0] - 1)
    return small(pair_kernel, [], [own, got], outs)


def folded(flags, blocks, states, head):
    closed = jnp.zeros((HD, HD), jnp.float32)
    opened = flags[0].astype(jnp.float32) * states[0, head]
    for i in range(1, states.shape[0]):
        flag = flags[i].astype(jnp.float32)
        advance = (blocks[i - 1] < blocks[i]).astype(jnp.float32)
        closed, opened = (
            closed + advance * opened,
            flag * states[i, head] + (1.0 - advance) * opened,
        )
    return closed, opened


def joined(earlier, later, advance):
    return (
        earlier[0] + later[0] + advance * earlier[1],
        later[1] + (1.0 - advance) * earlier[1],
    )


def fold_kernel(flags, blocks, mine_ref, *rest):
    got_refs, (states_ref, carry_ref) = rest[:-2], rest[-2:]
    total = mine_ref[...]
    for got in got_refs:
        total = total + got[...].astype(jnp.float32)
    states_ref[...] = total
    for head in range(states_ref.shape[1]):
        closed, opened = folded(flags, blocks, states_ref, head)
        carry_ref[0, head] = closed.astype(jnp.bfloat16)
        carry_ref[1, head] = opened.astype(jnp.bfloat16)


def fold_states(flags, blocks, mine, got):
    outs = [
        jax.ShapeDtypeStruct(mine.shape, jnp.float32),
        jax.ShapeDtypeStruct((2,) + mine.shape[1:], jnp.bfloat16),
    ]
    return small(fold_kernel, [flags, blocks], [mine, *got], outs)


def join_kernel(has_prefix, sends, flags, blocks, near, far, states_ref, *rest):
    rest = list(rest)
    prefix_ref = rest.pop(0) if has_prefix else None
    got_ref = rest.pop(0)
    kept_ref = rest.pop(0) if has_prefix and sends else None
    out_ref = rest.pop(0)
    frames = states_ref.shape[0]
    before = near[frames - 1]
    for head in range(states_ref.shape[1]):
        prefix = (got_ref[0, head].astype(jnp.float32), got_ref[1, head].astype(jnp.float32))
        if has_prefix:
            advance = (far[frames - 1] < before).astype(jnp.float32)
            nearer = (
                prefix_ref[0, head].astype(jnp.float32),
                prefix_ref[1, head].astype(jnp.float32),
            )
            prefix = joined(prefix, nearer, advance)
        if sends:
            if has_prefix:
                kept_ref[0, head], kept_ref[1, head] = prefix
            advance = (before < blocks[frames - 1]).astype(jnp.float32)
            total = joined(prefix, folded(flags, blocks, states_ref, head), advance)
            out_ref[0, head] = total[0].astype(jnp.bfloat16)
            out_ref[1, head] = total[1].astype(jnp.bfloat16)
        else:
            closed, opened = prefix
            last = before
            for i in range(frames):
                flag = flags[i].astype(jnp.float32)
                advance = (last < blocks[i]).astype(jnp.float32)
                state = states_ref[i, head]
                read = closed + jnp.maximum(advance, flag) * opened + state
                out_ref[i, head] = read.astype(jnp.bfloat16)
                closed = closed + advance * opened
                opened = flag * state + (1.0 - advance) * opened
                last = blocks[i]


def join(flags, blocks, near, far, states, prefix, got, sends):
    arrays = [states] + ([] if prefix is None else [prefix]) + [got]
    outs = []
    if sends and prefix is not None:
        outs.append(jax.ShapeDtypeStruct(got.shape, jnp.float32))
    shape = got.shape if sends else states.shape
    outs.append(jax.ShapeDtypeStruct(shape, jnp.bfloat16))
    body = functools.partial(join_kernel, prefix is not None, sends)
    return small(body, [flags, blocks, near, far], arrays, outs)


def bands(width):
    edges = list(range(0, width, BAND)) + [width]
    return [slice(*pair) for pair in zip(edges, edges[1:])]


def project_kernel(chunks, pieces, table_of, q_ref, gain_ref, *rest):
    state_refs = rest[:chunks]
    weight_refs = rest[chunks : chunks + pieces]
    out_ref, states, weight, turned, normed, out, state_sem, out_sem = rest[chunks + pieces :]
    frames, lat_rows, width, lat_cols = q_ref.shape
    tokens = lat_rows * lat_cols
    heads_per = states.shape[2]
    held, offsets = table_of(*(lax.axis_index(name) for name in ("grp", "frm", "row")))
    state_copies = [
        pltpu.make_async_copy(state_refs[n], states.at[held[n]], state_sem.at[n])
        for n in range(chunks)
    ]
    for copy in state_copies:
        copy.start()
    for ref, (row, column) in zip(weight_refs, offsets):
        at = pl.ds(pl.multiple_of(row, 16), ref.shape[0])
        weight[at, pl.ds(pl.multiple_of(column, LANES), ref.shape[1])] = ref[...]
    for copy in state_copies:
        copy.wait()
    gains = gain_ref[...].T
    for head in range(HEADS):
        chunk, slot = divmod(head, heads_per)
        at = slice(head * HD, (head + 1) * HD)
        gain = gains[:, head : head + 1]
        for frame in range(frames):
            attended = jnp.dot(
                states[chunk, frame, slot],
                jnp.maximum(side_by_side(q_ref, frame, at), 0),
                preferred_element_type=jnp.float32,
            )
            mean = jnp.mean(attended * attended, axis=0, keepdims=True)
            scaled = attended * lax.rsqrt(mean + norm_eps) * gain
            turned[at, frame * tokens : (frame + 1) * tokens] = scaled.astype(jnp.bfloat16)
    for start in range(0, width, 256):
        at = slice(start, min(start + 256, width))
        normed[:, at] = turned[at, :].T
    stores = []
    for b, band in enumerate(bands(width)):
        for start in range(band.start, band.stop, 256):
            at = slice(start, min(start + 256, band.stop))
            result = jnp.dot(normed[...], weight[:, at], preferred_element_type=jnp.float32)
            result = result.astype(jnp.bfloat16).T
            for frame in range(frames):
                for r in range(lat_rows):
                    first = frame * tokens + r * lat_cols
                    out[frame, r, at, :] = result[:, first : first + lat_cols]
        stores.append(
            pltpu.make_async_copy(out.at[:, :, band], out_ref.at[:, :, band], out_sem.at[b])
        )
        stores[-1].start()
    for store in stores:
        store.wait()


def project(queries, gain, states, weights, table_of):
    chunks, pieces = len(states), len(weights)
    frames, lat_rows, width, lat_cols = queries.shape
    tokens = frames * lat_rows * lat_cols
    anywhere = pl.BlockSpec(memory_space=pl.ANY)
    far = pl.BlockSpec(memory_space=pltpu.MemorySpace.HBM)
    whole = pl.BlockSpec(memory_space=pltpu.VMEM)
    count = len(bands(width))
    return pl.pallas_call(
        functools.partial(project_kernel, chunks, pieces, table_of),
        in_specs=[whole, whole] + [anywhere] * chunks + [whole] * pieces,
        out_specs=far,
        scratch_shapes=[
            pltpu.VMEM((chunks,) + states[0].shape, jnp.bfloat16),
            pltpu.VMEM((width, -(-width // LANES) * LANES), jnp.bfloat16),
            pltpu.VMEM((width, tokens), jnp.bfloat16),
            pltpu.VMEM((tokens, width), jnp.bfloat16),
            pltpu.VMEM(queries.shape, jnp.bfloat16),
            pltpu.SemaphoreType.DMA((chunks,)),
            pltpu.SemaphoreType.DMA((count,)),
        ],
        out_shape=jax.ShapeDtypeStruct(queries.shape, jnp.bfloat16),
        cost_estimate=pl.CostEstimate(
            flops=2 * queries.size * (width + 4 * HD),
            bytes_accessed=2 * (2 * queries.size + width * width),
            transcendentals=0,
        ),
        compiler_params=pltpu.CompilerParams(vmem_limit_bytes=PROJECT_VMEM),
        name="project",
    )(queries, gain, *states, *weights)


def gather_weight(weight, sizes, places):
    groups, frms, rows = sizes
    grp, _, row = places
    own_rows, width = weight.shape
    chips = rows // 2
    members = groups * chips
    half = -(-width // (2 * LANES)) * LANES
    piece_rows = -(-own_rows // (16 * members)) * 16
    if own_rows % 16 or piece_rows > own_rows or half >= width:
        whole = lax.all_gather(weight, "frm", axis=0, tiled=True)
        return [whole], lambda grp, frm, row: [(frm * 0, frm * 0)]

    def first_row(number):
        over = members * piece_rows - own_rows
        assert over < piece_rows
        return number * piece_rows - (number + 1) // members * over

    start = first_row(grp * chips + row // 2)
    lines = lax.dynamic_slice_in_dim(weight, start, piece_rows, 0)
    right = jnp.pad(lines[:, half:], ((0, 0), (0, 2 * half - width)))
    piece = jnp.where(row % 2 == 0, lines[:, :half], right)
    arrays, plan, reached = [weight], [], {}
    cores = [(i, i ^ 1) for i in range(rows)]
    order = sorted(range(1, frms), key=lambda s: min(s, frms - s))
    for turn, shift in enumerate(order):
        hop = 1 if 2 * shift <= frms else -1
        behind = reached.get(shift - hop, piece)
        first = lax.ppermute(behind, "frm", ring(frms, hop))
        reached[shift] = first
        held = {(0, 0): first}
        for axis in ("row", "grp") if turn else ("grp", "row"):
            for (dg, dx), block in list(held.items()):
                if axis == "grp":
                    for s in range(1, groups):
                        held[(dg + s, dx)] = lax.ppermute(block, "grp", ring(groups, s))
                else:
                    for s in range(1, chips):
                        held[(dg, dx + s)] = lax.ppermute(block, "row", ring(rows, 2 * s))
        for (dg, dx), block in held.items():
            arrays.append(block)
            arrays.append(lax.ppermute(block, "row", cores))
            plan.append((shift, dg, dx))

    def offsets(grp, frm, row):
        chip, core = row // 2, lax.rem(row, 2)
        starts = [(frm * own_rows, frm * 0)]
        for shift, dg, dx in plan:
            base = lax.rem(frm + frms - shift, frms) * own_rows
            g, x = lax.rem(grp + groups - dg, groups), lax.rem(chip + chips - dx, chips)
            at = base + first_row(g * chips + x)
            starts += [(at, core * half), (at, (1 - core) * half)]
        return starts

    return arrays, offsets


def local(sizes, *args):
    return attention(sizes, *args)


def attention(sizes, queries, keys, values, flags, blocks, out_weight, norm_gain):
    _, frms, rows = sizes
    chips = rows // 2
    places = tuple(lax.axis_index(name) for name in ("grp", "frm", "row"))
    heads_per = -(-HEADS // rows)
    queries, keys, values = (a.transpose(0, 1, 3, 2) for a in (queries, keys, values))
    cores = [(i, i ^ 1) for i in range(rows)]

    def chip_pairs(step):
        return [(i, (i + 2 * step) % rows) for i in range(rows)]

    def ahead(reach):
        return [(i, i + reach) for i in range(frms - reach)]

    weights, offsets_of = gather_weight(out_weight, sizes, places)

    own, sent = partial_states(keys, values, rows, heads_per)
    mine, *sends = add_pair(own, lax.ppermute(sent, "row", cores))
    got = [lax.ppermute(a, "row", chip_pairs(s)) for s, a in enumerate(sends, 1)]
    near = lax.ppermute(blocks, "frm", ahead(1))
    states, carry = fold_states(flags, blocks, mine, got)

    prefix, reach, far = None, 1, near
    while True:
        got = lax.ppermute(carry, "frm", ahead(reach))
        last = 2 * reach >= frms
        out = join(flags, blocks, near, far, states, prefix, got, not last)
        if last:
            read = out[0]
            break
        carry = out[-1]
        prefix = got if prefix is None else out[0]
        reach *= 2
        far = lax.ppermute(blocks, "frm", ahead(reach))

    shared = [read]
    for step in range(1, chips):
        shared.append(lax.ppermute(read, "row", chip_pairs(step)))
    reads = []
    for array in shared:
        reads += [array, lax.ppermute(array, "row", cores)]

    def table_of(grp, frm, row):
        chip, core = row // 2, lax.rem(row, 2)
        held = []
        for step in range(chips):
            other = lax.rem(chip + chips - step, chips) * 2
            held += [other + core, other + 1 - core]
        return held, offsets_of(grp, frm, row)

    gains = norm_gain.reshape(HEADS, HD)
    projected = project(queries, gains, reads, weights, table_of)
    return projected.transpose(0, 1, 3, 2)


def solution(mesh):
    sizes = tuple(mesh.shape[name] for name in ("grp", "frm", "row"))
    in_specs = (
        P(("grp", "frm"), "row", None, None),
        P(("grp", "frm"), "row", None, None),
        P(("grp", "frm"), "row", None, None),
        P(("grp", "frm")),
        P(("grp", "frm")),
        P("frm", None),
        P(),
    )
    out_specs = P(("grp", "frm"), "row", None, None)
    return jax.shard_map(
        functools.partial(local, sizes),
        mesh=mesh,
        in_specs=in_specs,
        out_specs=out_specs,
        check_vma=False,
    )
```

```python
import functools

import jax
import jax.numpy as jnp
from jax import lax
from jax.experimental import pallas as pl
from jax.experimental.pallas import tpu as pltpu
from jax.sharding import PartitionSpec as P


HEADS = 20
HD = 112

norm_eps = 1e-06

STATES_VMEM = 63500000
CUT_VMEM = 63500000
SMALL_VMEM = 8 << 20
PROJECT_VMEM = 36 << 20
LANES = 128
LOADS = 4
BAND = 768


def ring(size, shift):
    return [(i, (i + shift) % size) for i in range(size)]


def side_by_side(ref, frame, rows):
    return jnp.concatenate([ref[frame, r, rows, :] for r in range(ref.shape[1])], axis=1)


def state_kernel(chips, heads_per, k_ref, v_ref, own_ref, sent_ref, *scratch):
    keys, values, exact, rounded, load_sem, sem = scratch
    row = lax.axis_index("row")
    chip, core = row // 2, lax.rem(row, 2)
    frames, _, width, _ = keys.shape
    per = width // LOADS
    loads = []
    for frame in range(frames):
        for part in range(LOADS):
            at = pl.ds(part * per, per)
            loads.append(
                [
                    pltpu.make_async_copy(
                        ref.at[frame, :, at], held.at[frame, :, at], load_sem.at[n, frame, part]
                    )
                    for n, (ref, held) in enumerate(((k_ref, keys), (v_ref, values)))
                ]
            )
    for pair in loads:
        for load in pair:
            load.start()
    for frame in range(frames):
        for head in range(HEADS):
            if head * HD % per == 0:
                for load in loads[frame * LOADS + head * HD // per]:
                    load.wait()
            at = slice(head * HD, (head + 1) * HD)
            state = lax.dot_general(
                side_by_side(values, frame, at),
                jnp.maximum(side_by_side(keys, frame, at), 0),
                (((1,), (1,)), ((), ())),
                preferred_element_type=jnp.float32,
            )
            exact[frame, head] = state
            rounded[frame, head] = state.astype(jnp.bfloat16)
        for head in range(HEADS, exact.shape[1]):
            exact[frame, head] = jnp.zeros((HD, HD), jnp.float32)
            rounded[frame, head] = jnp.zeros((HD, HD), jnp.bfloat16)
    copies = []
    for frame in range(frames):
        for step in range(chips):
            other = lax.rem(chip + step, chips) * 2
            mine = pl.ds((other + core) * heads_per, heads_per)
            theirs = pl.ds((other + 1 - core) * heads_per, heads_per)
            copies.append(
                pltpu.make_async_copy(
                    rounded.at[frame, theirs], sent_ref.at[step, frame], sem.at[1, frame, step]
                )
            )
            copies.append(
                pltpu.make_async_copy(
                    exact.at[frame, mine], own_ref.at[step, frame], sem.at[0, frame, step]
                )
            )
    for copy in copies:
        copy.start()
    for copy in copies:
        copy.wait()


def partial_states(keys, values, rows, heads_per):
    frames, _, _, _ = keys.shape
    chips = rows // 2
    far = pl.BlockSpec(memory_space=pltpu.MemorySpace.HBM)
    anywhere = pl.BlockSpec(memory_space=pl.ANY)
    piece = (chips, frames, heads_per, HD, HD)
    held = (frames, rows * heads_per, HD, HD)
    return pl.pallas_call(
        functools.partial(state_kernel, chips, heads_per),
        in_specs=[far, far],
        out_specs=[anywhere] * 2,
        scratch_shapes=[
            pltpu.VMEM(keys.shape, jnp.bfloat16),
            pltpu.VMEM(keys.shape, jnp.bfloat16),
            pltpu.VMEM(held, jnp.float32),
            pltpu.VMEM(held, jnp.bfloat16),
            pltpu.SemaphoreType.DMA((2, frames, LOADS)),
            pltpu.SemaphoreType.DMA((2, frames, chips)),
        ],
        out_shape=[
            jax.ShapeDtypeStruct(piece, jnp.float32),
            jax.ShapeDtypeStruct(piece, jnp.bfloat16),
        ],
        cost_estimate=pl.CostEstimate(
            flops=2 * keys.size * HD * 8, bytes_accessed=4 * keys.size, transcendentals=0
        ),
        compiler_params=pltpu.CompilerParams(vmem_limit_bytes=STATES_VMEM),
        name="states",
    )(keys, values)


def small(body, scalars, arrays, outs):
    scalar = pl.BlockSpec(memory_space=pltpu.SMEM)
    whole = pl.BlockSpec(memory_space=pltpu.VMEM)
    moved_bytes = sum(a.size * a.dtype.itemsize for a in arrays)
    return pl.pallas_call(
        body,
        in_specs=[scalar] * len(scalars) + [whole] * len(arrays),
        out_specs=[whole] * len(outs),
        out_shape=outs,
        cost_estimate=pl.CostEstimate(
            flops=moved_bytes, bytes_accessed=2 * moved_bytes, transcendentals=0
        ),
        compiler_params=pltpu.CompilerParams(vmem_limit_bytes=SMALL_VMEM),
    )(*scalars, *arrays)


def pair_kernel(own_ref, got_ref, mine_ref, *sent_refs):
    mine_ref[...] = own_ref[0] + got_ref[0].astype(jnp.float32)
    for step, sent_ref in enumerate(sent_refs, 1):
        total = own_ref[step] + got_ref[step].astype(jnp.float32)
        sent_ref[...] = total.astype(jnp.bfloat16)


def add_pair(own, got):
    shape = own.shape[1:]
    outs = [jax.ShapeDtypeStruct(shape, jnp.float32)]
    outs += [jax.ShapeDtypeStruct(shape, jnp.bfloat16)] * (own.shape[0] - 1)
    return small(pair_kernel, [], [own, got], outs)


def folded(flags, blocks, states, head):
    closed = jnp.zeros((HD, HD), jnp.float32)
    opened = flags[0].astype(jnp.float32) * states[0, head]
    for i in range(1, states.shape[0]):
        flag = flags[i].astype(jnp.float32)
        advance = (blocks[i - 1] < blocks[i]).astype(jnp.float32)
        closed, opened = (
            closed + advance * opened,
            flag * states[i, head] + (1.0 - advance) * opened,
        )
    return closed, opened


def joined(earlier, later, advance):
    return (
        earlier[0] + later[0] + advance * earlier[1],
        later[1] + (1.0 - advance) * earlier[1],
    )


def fold_kernel(flags, blocks, mine_ref, *rest):
    got_refs, (states_ref, carry_ref) = rest[:-2], rest[-2:]
    total = mine_ref[...]
    for got in got_refs:
        total = total + got[...].astype(jnp.float32)
    states_ref[...] = total
    for head in range(states_ref.shape[1]):
        closed, opened = folded(flags, blocks, states_ref, head)
        carry_ref[0, head] = closed.astype(jnp.bfloat16)
        carry_ref[1, head] = opened.astype(jnp.bfloat16)


def fold_states(flags, blocks, mine, got):
    outs = [
        jax.ShapeDtypeStruct(mine.shape, jnp.float32),
        jax.ShapeDtypeStruct((2,) + mine.shape[1:], jnp.bfloat16),
    ]
    return small(fold_kernel, [flags, blocks], [mine, *got], outs)


def join_kernel(has_prefix, sends, flags, blocks, near, far, states_ref, *rest):
    rest = list(rest)
    prefix_ref = rest.pop(0) if has_prefix else None
    got_ref = rest.pop(0)
    kept_ref = rest.pop(0) if has_prefix and sends else None
    out_ref = rest.pop(0)
    frames = states_ref.shape[0]
    before = near[frames - 1]
    for head in range(states_ref.shape[1]):
        prefix = (got_ref[0, head].astype(jnp.float32), got_ref[1, head].astype(jnp.float32))
        if has_prefix:
            advance = (far[frames - 1] < before).astype(jnp.float32)
            nearer = (
                prefix_ref[0, head].astype(jnp.float32),
                prefix_ref[1, head].astype(jnp.float32),
            )
            prefix = joined(prefix, nearer, advance)
        if sends:
            if has_prefix:
                kept_ref[0, head], kept_ref[1, head] = prefix
            advance = (before < blocks[frames - 1]).astype(jnp.float32)
            total = joined(prefix, folded(flags, blocks, states_ref, head), advance)
            out_ref[0, head] = total[0].astype(jnp.bfloat16)
            out_ref[1, head] = total[1].astype(jnp.bfloat16)
        else:
            closed, opened = prefix
            last = before
            for i in range(frames):
                flag = flags[i].astype(jnp.float32)
                advance = (last < blocks[i]).astype(jnp.float32)
                state = states_ref[i, head]
                read = closed + jnp.maximum(advance, flag) * opened + state
                out_ref[i, head] = read.astype(jnp.bfloat16)
                closed = closed + advance * opened
                opened = flag * state + (1.0 - advance) * opened
                last = blocks[i]


def join(flags, blocks, near, far, states, prefix, got, sends):
    arrays = [states] + ([] if prefix is None else [prefix]) + [got]
    outs = []
    if sends and prefix is not None:
        outs.append(jax.ShapeDtypeStruct(got.shape, jnp.float32))
    shape = got.shape if sends else states.shape
    outs.append(jax.ShapeDtypeStruct(shape, jnp.bfloat16))
    body = functools.partial(join_kernel, prefix is not None, sends)
    return small(body, [flags, blocks, near, far], arrays, outs)


def bands(width):
    edges = list(range(0, width, BAND)) + [width]
    return [slice(*pair) for pair in zip(edges, edges[1:])]


def project_kernel(chunks, pieces, table_of, q_ref, gain_ref, *rest):
    state_refs = rest[:chunks]
    weight_refs = rest[chunks : chunks + pieces]
    out_ref, states, weight, turned, normed, out, state_sem, out_sem = rest[chunks + pieces :]
    frames, lat_rows, width, lat_cols = q_ref.shape
    tokens = lat_rows * lat_cols
    heads_per = states.shape[2]
    held, offsets = table_of(*(lax.axis_index(name) for name in ("grp", "frm", "row")))
    state_copies = [
        pltpu.make_async_copy(state_refs[n], states.at[held[n]], state_sem.at[n])
        for n in range(chunks)
    ]
    for copy in state_copies:
        copy.start()
    for ref, (row, column) in zip(weight_refs, offsets):
        at = pl.ds(pl.multiple_of(row, 16), ref.shape[0])
        weight[at, pl.ds(pl.multiple_of(column, LANES), ref.shape[1])] = ref[...]
    for copy in state_copies:
        copy.wait()
    gains = gain_ref[...].T
    for head in range(HEADS):
        chunk, slot = divmod(head, heads_per)
        at = slice(head * HD, (head + 1) * HD)
        gain = gains[:, head : head + 1]
        for frame in range(frames):
            attended = jnp.dot(
                states[chunk, frame, slot],
                jnp.maximum(side_by_side(q_ref, frame, at), 0),
                preferred_element_type=jnp.float32,
            )
            mean = jnp.mean(attended * attended, axis=0, keepdims=True)
            scaled = attended * lax.rsqrt(mean + norm_eps) * gain
            turned[at, frame * tokens : (frame + 1) * tokens] = scaled.astype(jnp.bfloat16)
    for start in range(0, width, 256):
        at = slice(start, min(start + 256, width))
        normed[:, at] = turned[at, :].T
    stores = []
    for b, band in enumerate(bands(width)):
        for start in range(band.start, band.stop, 256):
            at = slice(start, min(start + 256, band.stop))
            result = jnp.dot(normed[...], weight[:, at], preferred_element_type=jnp.float32)
            result = result.astype(jnp.bfloat16).T
            for frame in range(frames):
                for r in range(lat_rows):
                    first = frame * tokens + r * lat_cols
                    out[frame, r, at, :] = result[:, first : first + lat_cols]
        stores.append(
            pltpu.make_async_copy(out.at[:, :, band], out_ref.at[:, :, band], out_sem.at[b])
        )
        stores[-1].start()
    for store in stores:
        store.wait()


def project(queries, gain, states, weights, table_of):
    chunks, pieces = len(states), len(weights)
    frames, lat_rows, width, lat_cols = queries.shape
    tokens = frames * lat_rows * lat_cols
    anywhere = pl.BlockSpec(memory_space=pl.ANY)
    far = pl.BlockSpec(memory_space=pltpu.MemorySpace.HBM)
    whole = pl.BlockSpec(memory_space=pltpu.VMEM)
    count = len(bands(width))
    return pl.pallas_call(
        functools.partial(project_kernel, chunks, pieces, table_of),
        in_specs=[whole, whole] + [anywhere] * chunks + [whole] * pieces,
        out_specs=far,
        scratch_shapes=[
            pltpu.VMEM((chunks,) + states[0].shape, jnp.bfloat16),
            pltpu.VMEM((width, -(-width // LANES) * LANES), jnp.bfloat16),
            pltpu.VMEM((width, tokens), jnp.bfloat16),
            pltpu.VMEM((tokens, width), jnp.bfloat16),
            pltpu.VMEM(queries.shape, jnp.bfloat16),
            pltpu.SemaphoreType.DMA((chunks,)),
            pltpu.SemaphoreType.DMA((count,)),
        ],
        out_shape=jax.ShapeDtypeStruct(queries.shape, jnp.bfloat16),
        cost_estimate=pl.CostEstimate(
            flops=2 * queries.size * (width + 4 * HD),
            bytes_accessed=2 * (2 * queries.size + width * width),
            transcendentals=0,
        ),
        compiler_params=pltpu.CompilerParams(vmem_limit_bytes=PROJECT_VMEM),
        name="project",
    )(queries, gain, *states, *weights)


def cut_kernel(chips, members, weight_ref, piece_ref, lines, sem):
    row = lax.axis_index("row")
    number = lax.axis_index("grp") * chips + row // 2
    count, half = piece_ref.shape
    over = members * count - weight_ref.shape[0]
    start = pl.multiple_of(number * count - (number + 1) // members * over, 16)
    copy = pltpu.make_async_copy(weight_ref.at[pl.ds(start, count)], lines, sem)
    copy.start()
    copy.wait()

    @pl.when(lax.rem(row, 2) == 0)
    def _():
        piece_ref[...] = lines[:, :half]

    @pl.when(lax.rem(row, 2) == 1)
    def _():
        rest = lines.shape[1] - half
        full = rest // LANES * LANES
        piece_ref[:, :full] = lines[:, half : half + full]
        if full < half:
            blank = jnp.zeros((count, half - rest), lines.dtype)
            piece_ref[:, full:] = jnp.concatenate([lines[:, half + full :], blank], axis=1)


def cut_piece(weight, groups, chips, piece_rows, half):
    return pl.pallas_call(
        functools.partial(cut_kernel, chips, groups * chips),
        in_specs=[pl.BlockSpec(memory_space=pl.ANY)],
        out_specs=pl.BlockSpec(memory_space=pltpu.VMEM),
        out_shape=jax.ShapeDtypeStruct((piece_rows, half), weight.dtype),
        scratch_shapes=[
            pltpu.VMEM((piece_rows, weight.shape[1]), weight.dtype),
            pltpu.SemaphoreType.DMA,
        ],
        compiler_params=pltpu.CompilerParams(vmem_limit_bytes=CUT_VMEM),
        name="cut",
    )(weight)


def gather_weight(weight, sizes, places):
    groups, frms, rows = sizes
    grp, frm, row = places
    own_rows, width = weight.shape
    chips = rows // 2
    members = groups * chips
    half = -(-width // (2 * LANES)) * LANES
    piece_rows = -(-own_rows // (16 * members)) * 16
    if own_rows % 16 or piece_rows > own_rows or half >= width:
        whole = lax.all_gather(weight, "frm", axis=0, tiled=True)
        return [whole], lambda grp, frm, row: [(frm * 0, frm * 0)]

    def first_row(number):
        over = members * piece_rows - own_rows
        return number * piece_rows - (number + 1) // members * over

    piece = cut_piece(weight, groups, chips, piece_rows, half)
    arrays, plan, reached = [weight], [], {}
    cores = [(i, i ^ 1) for i in range(rows)]
    order = sorted(range(1, frms), key=lambda s: min(s, frms - s))
    for turn, shift in enumerate(order):
        hop = 1 if 2 * shift <= frms else -1
        behind = reached.get(shift - hop, piece)
        first = lax.ppermute(behind, "frm", ring(frms, hop))
        reached[shift] = first
        held = {(0, 0): first}
        for axis in ("row", "grp") if turn else ("grp", "row"):
            for (dg, dx), block in list(held.items()):
                if axis == "grp":
                    for s in range(1, groups):
                        held[(dg + s, dx)] = lax.ppermute(block, "grp", ring(groups, s))
                else:
                    for s in range(1, chips):
                        held[(dg, dx + s)] = lax.ppermute(block, "row", ring(rows, 2 * s))
        for (dg, dx), block in held.items():
            arrays.append(block)
            arrays.append(lax.ppermute(block, "row", cores))
            plan.append((shift, dg, dx))

    def offsets(grp, frm, row):
        chip, core = row // 2, lax.rem(row, 2)
        starts = [(frm * own_rows, frm * 0)]
        for shift, dg, dx in plan:
            base = lax.rem(frm + frms - shift, frms) * own_rows
            g, x = lax.rem(grp + groups - dg, groups), lax.rem(chip + chips - dx, chips)
            at = base + first_row(g * chips + x)
            starts += [(at, core * half), (at, (1 - core) * half)]
        return starts

    return arrays, offsets


def local(sizes, *args):
    return attention(sizes, *args)


def attention(sizes, queries, keys, values, flags, blocks, out_weight, norm_gain):
    _, frms, rows = sizes
    chips = rows // 2
    places = tuple(lax.axis_index(name) for name in ("grp", "frm", "row"))
    heads_per = -(-HEADS // rows)
    queries, keys, values = (a.transpose(0, 1, 3, 2) for a in (queries, keys, values))
    cores = [(i, i ^ 1) for i in range(rows)]

    def chip_pairs(step):
        return [(i, (i + 2 * step) % rows) for i in range(rows)]

    def ahead(reach):
        return [(i, i + reach) for i in range(frms - reach)]

    weights, offsets_of = gather_weight(out_weight, sizes, places)

    own, sent = partial_states(keys, values, rows, heads_per)
    mine, *sends = add_pair(own, lax.ppermute(sent, "row", cores))
    got = [lax.ppermute(a, "row", chip_pairs(s)) for s, a in enumerate(sends, 1)]
    near = lax.ppermute(blocks, "frm", ahead(1))
    states, carry = fold_states(flags, blocks, mine, got)

    prefix, reach, far = None, 1, near
    while True:
        got = lax.ppermute(carry, "frm", ahead(reach))
        last = 2 * reach >= frms
        out = join(flags, blocks, near, far, states, prefix, got, not last)
        if last:
            read = out[0]
            break
        carry = out[-1]
        prefix = got if prefix is None else out[0]
        reach *= 2
        far = lax.ppermute(blocks, "frm", ahead(reach))

    shared = [read]
    for step in range(1, chips):
        shared.append(lax.ppermute(read, "row", chip_pairs(step)))
    reads = []
    for array in shared:
        reads += [array, lax.ppermute(array, "row", cores)]

    def table_of(grp, frm, row):
        chip, core = row // 2, lax.rem(row, 2)
        held = []
        for step in range(chips):
            other = lax.rem(chip + chips - step, chips) * 2
            held += [other + core, other + 1 - core]
        return held, offsets_of(grp, frm, row)

    gains = norm_gain.reshape(HEADS, HD)
    projected = project(queries, gains, reads, weights, table_of)
    return projected.transpose(0, 1, 3, 2)


def solution(mesh):
    sizes = tuple(mesh.shape[name] for name in ("grp", "frm", "row"))
    in_specs = (
        P(("grp", "frm"), "row", None, None),
        P(("grp", "frm"), "row", None, None),
        P(("grp", "frm"), "row", None, None),
        P(("grp", "frm")),
        P(("grp", "frm")),
        P("frm", None),
        P(),
    )
    out_specs = P(("grp", "frm"), "row", None, None)
    return jax.shard_map(
        functools.partial(local, sizes),
        mesh=mesh,
        in_specs=in_specs,
        out_specs=out_specs,
        check_vma=False,
    )
```

```python
import functools

import jax
import jax.numpy as jnp
from jax import lax
from jax.experimental import pallas as pl
from jax.experimental.pallas import tpu as pltpu
from jax.sharding import PartitionSpec as P


HEADS = 20
HD = 112

norm_eps = 1e-06

STATES_VMEM = 63500000
CUT_VMEM = 63500000
SMALL_VMEM = 8 << 20
PROJECT_VMEM = 36 << 20
LANES = 128
SPARE = LANES - HD
STRIPS = HD // SPARE
LOADS = 4
BAND = 768


def ring(size, shift):
    return [(i, (i + shift) % size) for i in range(size)]


def side_by_side(ref, frame, rows):
    return jnp.concatenate([ref[frame, r, rows, :] for r in range(ref.shape[1])], axis=1)


def state_kernel(chips, heads_per, k_ref, v_ref, own_ref, sent_ref, *scratch):
    keys, values, exact, rounded, load_sem, sem = scratch
    row = lax.axis_index("row")
    chip, core = row // 2, lax.rem(row, 2)
    frames, _, width, _ = keys.shape
    per = width // LOADS
    loads = []
    for frame in range(frames):
        for part in range(LOADS):
            at = pl.ds(part * per, per)
            loads.append(
                [
                    pltpu.make_async_copy(
                        ref.at[frame, :, at], held.at[frame, :, at], load_sem.at[n, frame, part]
                    )
                    for n, (ref, held) in enumerate(((k_ref, keys), (v_ref, values)))
                ]
            )
    for pair in loads:
        for load in pair:
            load.start()
    for frame in range(frames):
        for head in range(HEADS):
            if head * HD % per == 0:
                for load in loads[frame * LOADS + head * HD // per]:
                    load.wait()
            at = slice(head * HD, (head + 1) * HD)
            state = lax.dot_general(
                side_by_side(values, frame, at),
                jnp.maximum(side_by_side(keys, frame, at), 0),
                (((1,), (1,)), ((), ())),
                preferred_element_type=jnp.float32,
            )
            exact[frame, head] = state
            rounded[frame, head] = state.astype(jnp.bfloat16)
        for head in range(HEADS, exact.shape[1]):
            exact[frame, head] = jnp.zeros((HD, HD), jnp.float32)
            rounded[frame, head] = jnp.zeros((HD, HD), jnp.bfloat16)
    copies = []
    for frame in range(frames):
        for step in range(chips):
            other = lax.rem(chip + step, chips) * 2
            mine = pl.ds((other + core) * heads_per, heads_per)
            theirs = pl.ds((other + 1 - core) * heads_per, heads_per)
            copies.append(
                pltpu.make_async_copy(
                    rounded.at[frame, theirs], sent_ref.at[step, frame], sem.at[1, frame, step]
                )
            )
            copies.append(
                pltpu.make_async_copy(
                    exact.at[frame, mine], own_ref.at[step, frame], sem.at[0, frame, step]
                )
            )
    for copy in copies:
        copy.start()
    for copy in copies:
        copy.wait()


def partial_states(keys, values, rows, heads_per):
    frames, _, _, _ = keys.shape
    chips = rows // 2
    far = pl.BlockSpec(memory_space=pltpu.MemorySpace.HBM)
    anywhere = pl.BlockSpec(memory_space=pl.ANY)
    piece = (chips, frames, heads_per, HD, HD)
    held = (frames, rows * heads_per, HD, HD)
    return pl.pallas_call(
        functools.partial(state_kernel, chips, heads_per),
        in_specs=[far, far],
        out_specs=[anywhere] * 2,
        scratch_shapes=[
            pltpu.VMEM(keys.shape, jnp.bfloat16),
            pltpu.VMEM(keys.shape, jnp.bfloat16),
            pltpu.VMEM(held, jnp.float32),
            pltpu.VMEM(held, jnp.bfloat16),
            pltpu.SemaphoreType.DMA((2, frames, LOADS)),
            pltpu.SemaphoreType.DMA((2, frames, chips)),
        ],
        out_shape=[
            jax.ShapeDtypeStruct(piece, jnp.float32),
            jax.ShapeDtypeStruct(piece, jnp.bfloat16),
        ],
        cost_estimate=pl.CostEstimate(
            flops=2 * keys.size * HD * 8, bytes_accessed=4 * keys.size, transcendentals=0
        ),
        compiler_params=pltpu.CompilerParams(vmem_limit_bytes=STATES_VMEM),
        name="states",
    )(keys, values)


def small(body, scalars, arrays, outs):
    scalar = pl.BlockSpec(memory_space=pltpu.SMEM)
    whole = pl.BlockSpec(memory_space=pltpu.VMEM)
    moved_bytes = sum(a.size * a.dtype.itemsize for a in arrays)
    return pl.pallas_call(
        body,
        in_specs=[scalar] * len(scalars) + [whole] * len(arrays),
        out_specs=[whole] * len(outs),
        out_shape=outs,
        cost_estimate=pl.CostEstimate(
            flops=moved_bytes, bytes_accessed=2 * moved_bytes, transcendentals=0
        ),
        compiler_params=pltpu.CompilerParams(vmem_limit_bytes=SMALL_VMEM),
    )(*scalars, *arrays)


def packs(count):
    return (count - 1) // (STRIPS + 1)


def packed_shape(count):
    return jax.ShapeDtypeStruct((count - packs(count), HD, LANES), jnp.bfloat16)


def pack(values, ref, tag=0.0):
    full = packs(len(values))
    for n in range(full):
        *kept, split = values[n * (STRIPS + 1) : (n + 1) * (STRIPS + 1)]
        for i, value in enumerate(kept):
            strip = split[:, i * SPARE : (i + 1) * SPARE]
            unit = jnp.concatenate([value, strip], axis=1)
            ref[n * STRIPS + i] = unit.astype(jnp.bfloat16)
    rest = jnp.full((HD, SPARE), tag, jnp.float32)
    for i, value in enumerate(values[full * (STRIPS + 1) :]):
        unit = jnp.concatenate([value, rest], axis=1)
        ref[full * STRIPS + i] = unit.astype(jnp.bfloat16)


def unpack(ref, count):
    units = [ref[i].astype(jnp.float32) for i in range(ref.shape[0])]
    values = []
    for n in range(packs(count)):
        group = units[n * STRIPS : (n + 1) * STRIPS]
        values += [unit[:, :HD] for unit in group]
        values.append(jnp.concatenate([unit[:, HD:] for unit in group], axis=1))
    return values + [unit[:, :HD] for unit in units[packs(count) * STRIPS :]]


def tag_of(ref):
    return ref[ref.shape[0] - 1, 0:1, HD : HD + 1].astype(jnp.float32)


def each(frames, heads):
    return [(frame, head) for frame in range(frames) for head in range(heads)]


def pair_kernel(own_ref, got_ref, mine_ref, *sent_refs):
    mine_ref[...] = own_ref[0] + got_ref[0].astype(jnp.float32)
    for step, sent_ref in enumerate(sent_refs, 1):
        totals = [
            own_ref[(step,) + at] + got_ref[(step,) + at].astype(jnp.float32)
            for at in each(*own_ref.shape[1:3])
        ]
        pack(totals, sent_ref)


def add_pair(own, got):
    shape = own.shape[1:]
    outs = [jax.ShapeDtypeStruct(shape, jnp.float32)]
    outs += [packed_shape(shape[0] * shape[1])] * (own.shape[0] - 1)
    return small(pair_kernel, [], [own, got], outs)


def folded(flags, blocks, states, head):
    closed = jnp.zeros((HD, HD), jnp.float32)
    opened = flags[0].astype(jnp.float32) * states[0, head]
    for i in range(1, states.shape[0]):
        flag = flags[i].astype(jnp.float32)
        advance = (blocks[i - 1] < blocks[i]).astype(jnp.float32)
        closed, opened = (
            closed + advance * opened,
            flag * states[i, head] + (1.0 - advance) * opened,
        )
    return closed, opened


def joined(earlier, later, advance):
    return (
        earlier[0] + later[0] + advance * earlier[1],
        later[1] + (1.0 - advance) * earlier[1],
    )


def fold_kernel(flags, blocks, mine_ref, *rest):
    got_refs, (states_ref, carry_ref) = rest[:-2], rest[-2:]
    frames, heads = mine_ref.shape[:2]
    totals = [mine_ref[at] for at in each(frames, heads)]
    for got in got_refs:
        totals = [a + b for a, b in zip(totals, unpack(got, frames * heads))]
    for at, total in zip(each(frames, heads), totals):
        states_ref[at] = total
    pairs = [folded(flags, blocks, states_ref, head) for head in range(heads)]
    last = blocks[frames - 1].astype(jnp.float32)
    pack([pair[0] for pair in pairs] + [pair[1] for pair in pairs], carry_ref, last)


def fold_states(flags, blocks, mine, got):
    outs = [jax.ShapeDtypeStruct(mine.shape, jnp.float32), packed_shape(2 * mine.shape[1])]
    return small(fold_kernel, [flags, blocks], [mine, *got], outs)


def join_kernel(has_kept, has_far, sends, flags, blocks, states_ref, near_ref, *rest):
    rest = list(rest)
    kept_ref = rest.pop(0) if has_kept else None
    far_ref = rest.pop(0) if has_far else None
    frames, heads = states_ref.shape[:2]
    near = tag_of(near_ref)

    def pairs_of(ref):
        values = unpack(ref, 2 * heads)
        return list(zip(values[:heads], values[heads:]))

    if has_kept:
        prefix = [(kept_ref[0, head], kept_ref[1, head]) for head in range(heads)]
    else:
        prefix = pairs_of(near_ref)
    if has_far:
        advance = (tag_of(far_ref) < near).astype(jnp.float32)
        prefix = [joined(a, b, advance) for a, b in zip(pairs_of(far_ref), prefix)]
    if sends:
        if has_far:
            kept_out = rest.pop(0)
            for head, pair in enumerate(prefix):
                kept_out[0, head], kept_out[1, head] = pair
        last = blocks[frames - 1].astype(jnp.float32)
        advance = (near < last).astype(jnp.float32)
        totals = [
            joined(pair, folded(flags, blocks, states_ref, head), advance)
            for head, pair in enumerate(prefix)
        ]
        pack([t[0] for t in totals] + [t[1] for t in totals], rest.pop(0), last)
        return
    reads, before = [], near
    for i in range(frames):
        block = blocks[i].astype(jnp.float32)
        flag = flags[i].astype(jnp.float32)
        advance = (before < block).astype(jnp.float32)
        for head, (closed, opened) in enumerate(prefix):
            state = states_ref[i, head]
            reads.append(closed + jnp.maximum(advance, flag) * opened + state)
            prefix[head] = (
                closed + advance * opened,
                flag * state + (1.0 - advance) * opened,
            )
        before = block
    pack(reads, rest.pop(0))


def join(flags, blocks, states, near, kept, far, sends):
    frames, heads = states.shape[:2]
    outs = []
    if sends and far is not None:
        outs.append(jax.ShapeDtypeStruct((2,) + states.shape[1:], jnp.float32))
    outs.append(packed_shape(2 * heads if sends else frames * heads))
    arrays = [states, near] + [a for a in (kept, far) if a is not None]
    body = functools.partial(join_kernel, kept is not None, far is not None, sends)
    return small(body, [flags, blocks], arrays, outs)


def bands(width):
    edges = list(range(0, width, BAND)) + [width]
    return [slice(*pair) for pair in zip(edges, edges[1:])]


def project_kernel(chunks, pieces, table_of, q_ref, gain_ref, *rest):
    state_refs = rest[:chunks]
    weight_refs = rest[chunks : chunks + pieces]
    out_ref, states, weight, turned, normed, out, out_sem = rest[chunks + pieces :]
    frames, lat_rows, width, lat_cols = q_ref.shape
    tokens = lat_rows * lat_cols
    heads_per = states.shape[1] // frames
    held, offsets = table_of(*(lax.axis_index(name) for name in ("grp", "frm", "row")))
    for ref, (row, column) in zip(weight_refs, offsets):
        at = pl.ds(pl.multiple_of(row, 16), ref.shape[0])
        weight[at, pl.ds(pl.multiple_of(column, LANES), ref.shape[1])] = ref[...]
    for ref, chunk in zip(state_refs, held):
        for i, value in enumerate(unpack(ref, states.shape[1])):
            states[chunk, i] = value.astype(jnp.bfloat16)
    gains = gain_ref[...].T
    for head in range(HEADS):
        chunk, slot = divmod(head, heads_per)
        at = slice(head * HD, (head + 1) * HD)
        gain = gains[:, head : head + 1]
        for frame in range(frames):
            attended = jnp.dot(
                states[chunk, frame * heads_per + slot],
                jnp.maximum(side_by_side(q_ref, frame, at), 0),
                preferred_element_type=jnp.float32,
            )
            mean = jnp.mean(attended * attended, axis=0, keepdims=True)
            scaled = attended * lax.rsqrt(mean + norm_eps) * gain
            turned[at, frame * tokens : (frame + 1) * tokens] = scaled.astype(jnp.bfloat16)
    for start in range(0, width, 256):
        at = slice(start, min(start + 256, width))
        normed[:, at] = turned[at, :].T
    stores = []
    for b, band in enumerate(bands(width)):
        for start in range(band.start, band.stop, 256):
            at = slice(start, min(start + 256, band.stop))
            result = jnp.dot(normed[...], weight[:, at], preferred_element_type=jnp.float32)
            result = result.astype(jnp.bfloat16).T
            for frame in range(frames):
                for r in range(lat_rows):
                    first = frame * tokens + r * lat_cols
                    out[frame, r, at, :] = result[:, first : first + lat_cols]
        stores.append(
            pltpu.make_async_copy(out.at[:, :, band], out_ref.at[:, :, band], out_sem.at[b])
        )
        stores[-1].start()
    for store in stores:
        store.wait()


def project(queries, gain, states, count, weights, table_of):
    chunks, pieces = len(states), len(weights)
    frames, lat_rows, width, lat_cols = queries.shape
    tokens = frames * lat_rows * lat_cols
    far = pl.BlockSpec(memory_space=pltpu.MemorySpace.HBM)
    whole = pl.BlockSpec(memory_space=pltpu.VMEM)
    return pl.pallas_call(
        functools.partial(project_kernel, chunks, pieces, table_of),
        in_specs=[whole, whole] + [whole] * (chunks + pieces),
        out_specs=far,
        scratch_shapes=[
            pltpu.VMEM((chunks, count, HD, HD), jnp.bfloat16),
            pltpu.VMEM((width, -(-width // LANES) * LANES), jnp.bfloat16),
            pltpu.VMEM((width, tokens), jnp.bfloat16),
            pltpu.VMEM((tokens, width), jnp.bfloat16),
            pltpu.VMEM(queries.shape, jnp.bfloat16),
            pltpu.SemaphoreType.DMA((len(bands(width)),)),
        ],
        out_shape=jax.ShapeDtypeStruct(queries.shape, jnp.bfloat16),
        cost_estimate=pl.CostEstimate(
            flops=2 * queries.size * (width + 4 * HD),
            bytes_accessed=2 * (2 * queries.size + width * width),
            transcendentals=0,
        ),
        compiler_params=pltpu.CompilerParams(vmem_limit_bytes=PROJECT_VMEM),
        name="project",
    )(queries, gain, *states, *weights)


def cut_kernel(chips, members, weight_ref, piece_ref, lines, sem):
    row = lax.axis_index("row")
    number = lax.axis_index("grp") * chips + row // 2
    count, half = piece_ref.shape
    over = members * count - weight_ref.shape[0]
    start = pl.multiple_of(number * count - (number + 1) // members * over, 16)
    copy = pltpu.make_async_copy(weight_ref.at[pl.ds(start, count)], lines, sem)
    copy.start()
    copy.wait()

    @pl.when(lax.rem(row, 2) == 0)
    def _():
        piece_ref[...] = lines[:, :half]

    @pl.when(lax.rem(row, 2) == 1)
    def _():
        rest = lines.shape[1] - half
        full = rest // LANES * LANES
        piece_ref[:, :full] = lines[:, half : half + full]
        if full < half:
            blank = jnp.zeros((count, half - rest), lines.dtype)
            piece_ref[:, full:] = jnp.concatenate([lines[:, half + full :], blank], axis=1)


def cut_piece(weight, groups, chips, piece_rows, half):
    return pl.pallas_call(
        functools.partial(cut_kernel, chips, groups * chips),
        in_specs=[pl.BlockSpec(memory_space=pl.ANY)],
        out_specs=pl.BlockSpec(memory_space=pltpu.VMEM),
        out_shape=jax.ShapeDtypeStruct((piece_rows, half), weight.dtype),
        scratch_shapes=[
            pltpu.VMEM((piece_rows, weight.shape[1]), weight.dtype),
            pltpu.SemaphoreType.DMA,
        ],
        compiler_params=pltpu.CompilerParams(vmem_limit_bytes=CUT_VMEM),
        name="cut",
    )(weight)


def gather_weight(weight, sizes, places):
    groups, frms, rows = sizes
    grp, frm, row = places
    own_rows, width = weight.shape
    chips = rows // 2
    members = groups * chips
    half = -(-width // (2 * LANES)) * LANES
    piece_rows = -(-own_rows // (16 * members)) * 16
    if own_rows % 16 or piece_rows > own_rows or half >= width:
        whole = lax.all_gather(weight, "frm", axis=0, tiled=True)
        return [whole], lambda grp, frm, row: [(frm * 0, frm * 0)]

    def first_row(number):
        over = members * piece_rows - own_rows
        return number * piece_rows - (number + 1) // members * over

    piece = cut_piece(weight, groups, chips, piece_rows, half)
    arrays, plan, reached = [weight], [], {}
    cores = [(i, i ^ 1) for i in range(rows)]
    order = sorted(range(1, frms), key=lambda s: min(s, frms - s))
    for turn, shift in enumerate(order):
        hop = 1 if 2 * shift <= frms else -1
        behind = reached.get(shift - hop, piece)
        first = lax.ppermute(behind, "frm", ring(frms, hop))
        reached[shift] = first
        held = {(0, 0): first}
        for axis in ("row", "grp") if turn else ("grp", "row"):
            for (dg, dx), block in list(held.items()):
                if axis == "grp":
                    for s in range(1, groups):
                        held[(dg + s, dx)] = lax.ppermute(block, "grp", ring(groups, s))
                else:
                    for s in range(1, chips):
                        held[(dg, dx + s)] = lax.ppermute(block, "row", ring(rows, 2 * s))
        for (dg, dx), block in held.items():
            arrays.append(block)
            arrays.append(lax.ppermute(block, "row", cores))
            plan.append((shift, dg, dx))

    def offsets(grp, frm, row):
        chip, core = row // 2, lax.rem(row, 2)
        starts = [(frm * own_rows, frm * 0)]
        for shift, dg, dx in plan:
            base = lax.rem(frm + frms - shift, frms) * own_rows
            g, x = lax.rem(grp + groups - dg, groups), lax.rem(chip + chips - dx, chips)
            at = base + first_row(g * chips + x)
            starts += [(at, core * half), (at, (1 - core) * half)]
        return starts

    return arrays, offsets


def local(sizes, *args):
    return attention(sizes, *args)


def attention(sizes, queries, keys, values, flags, blocks, out_weight, norm_gain):
    _, frms, rows = sizes
    chips = rows // 2
    places = tuple(lax.axis_index(name) for name in ("grp", "frm", "row"))
    heads_per, frames = -(-HEADS // rows), queries.shape[0]
    queries, keys, values = (a.transpose(0, 1, 3, 2) for a in (queries, keys, values))
    cores = [(i, i ^ 1) for i in range(rows)]

    def chip_pairs(step):
        return [(i, (i + 2 * step) % rows) for i in range(rows)]

    def ahead(reach):
        return [(i, i + reach) for i in range(frms - reach)]

    weights, offsets_of = gather_weight(out_weight, sizes, places)

    own, sent = partial_states(keys, values, rows, heads_per)
    mine, *sends = add_pair(own, lax.ppermute(sent, "row", cores))
    got = [lax.ppermute(a, "row", chip_pairs(s)) for s, a in enumerate(sends, 1)]
    states, carry = fold_states(flags, blocks, mine, got)

    near, kept, reach = None, None, 1
    while True:
        got = lax.ppermute(carry, "frm", ahead(reach))
        last = 2 * reach >= frms
        near, far = (got, None) if near is None else (near, got)
        out = join(flags, blocks, states, near, kept, far, not last)
        if last:
            read = out[0]
            break
        carry = out[-1]
        kept = out[0] if far is not None else None
        reach *= 2

    shared = [read]
    for step in range(1, chips):
        shared.append(lax.ppermute(read, "row", chip_pairs(step)))
    reads = []
    for array in shared:
        reads += [array, lax.ppermute(array, "row", cores)]

    def table_of(grp, frm, row):
        chip, core = row // 2, lax.rem(row, 2)
        held = []
        for step in range(chips):
            other = lax.rem(chip + chips - step, chips) * 2
            held += [other + core, other + 1 - core]
        return held, offsets_of(grp, frm, row)

    gains = norm_gain.reshape(HEADS, HD)
    projected = project(queries, gains, reads, frames * heads_per, weights, table_of)
    return projected.transpose(0, 1, 3, 2)


def solution(mesh):
    sizes = tuple(mesh.shape[name] for name in ("grp", "frm", "row"))
    in_specs = (
        P(("grp", "frm"), "row", None, None),
        P(("grp", "frm"), "row", None, None),
        P(("grp", "frm"), "row", None, None),
        P(("grp", "frm")),
        P(("grp", "frm")),
        P("frm", None),
        P(),
    )
    out_specs = P(("grp", "frm"), "row", None, None)
    return jax.shard_map(
        functools.partial(local, sizes),
        mesh=mesh,
        in_specs=in_specs,
        out_specs=out_specs,
        check_vma=False,
    )
```
